32 devices in a mesh: dp: 4 (over z), row: 4 (over x, core), col: 2 (over y).
Axes of the slice: x: 2, y: 2, z: 4, core: 2. Of those that a mesh axis runs over, the one named last changes fastest.
Arguments:
- tokens: bfloat16 [512, 4096], P('dp', 'row'), may hold values from -6 to 6
- cotangent: bfloat16 [512, 4096], P('dp', 'row'), may hold values from -6 to 6
- weight_in: bfloat16 [4096, 15360], P('row', 'col'), may hold values from -0.09375 to 0.09375
- weight_out: bfloat16 [4096, 15360], P('row', 'col'), may hold values from -0.046875 to 0.046875
Outputs:
- outputs: bfloat16 [512, 4096], P(('dp', 'col'), 'row')
- token_gradient: bfloat16 [512, 4096], P(('dp', 'col'), 'row')
- weight_in_gradient: float32 [4096, 15360], P('row', ('col', 'dp'))
- weight_out_gradient: float32 [4096, 15360], P('row', ('col', 'dp'))
The draws below stay inside these ranges and needn't reach their ends.
All inputs are finite; a program needn't handle non-finite values.
Results may differ from the reference program's by a relative error of at most 0.017.
Values may be sent and summed in bfloat16 or wider, within the bound.
A program may use at most 192 MiB of HBM per device.

```python
import jax
import jax.numpy as jnp
from jax import lax

D = 4096
FF = 15360
TOKG = 128
TOKENS = 512
N_DP = 4
N_ROW = 4
N_COL = 2


def shard_levels(own_key, shape, pieces, smallest, high):
    def one(position, shards_of):
        heights = jax.random.uniform(jax.random.fold_in(jax.random.fold_in(own_key, 6), position), (shards_of,), jnp.float32, smallest / len(pieces), high / len(pieces))
        return jnp.repeat(jnp.exp(heights), shape[position] // shards_of).reshape((-1,) + (1,) * (len(shape) - position - 1))

    factor_of = one(*pieces[0])
    for cut in pieces[1:]:
        factor_of = factor_of * one(*cut)
    return factor_of


def normal_values(own_key, shape, width, reach, pieces=(), kind=jnp.bfloat16):
    gain = shard_levels(own_key, shape, pieces, -0.22, 0.18) if pieces else 1.0
    entries = jax.random.normal(own_key, shape, jnp.float32) * width * gain
    return jnp.minimum(jnp.maximum(entries, -reach), reach).astype(kind)


def setup_inputs(seed: int = 0) -> dict:
    seeds = jax.random.split(jax.random.key(seed), 5)
    return {
        "tokens": normal_values(seeds[0], (TOKENS, D), 1.0, 6.0, ((0, 4), (1, 4))),
        "cotangent": normal_values(seeds[1], (TOKENS, D), 1.0, 6.0, ((0, 4), (1, 4))),
        "weight_in": normal_values(seeds[2], (D, FF), D ** -0.5, 0.09375, ((0, 4), (1, 2))),
        "weight_out": normal_values(seeds[3], (D, FF), FF ** -0.5, 0.046875, ((0, 4), (1, 2))),
    }


root_half = 0.7071067811865476
inv_root_tau = 0.3989422804014327


def gelu_pair(hidden):
    normal_cdf = 0.5 * (1.0 + lax.erf(hidden * root_half))
    density = jnp.exp(-0.5 * hidden * hidden) * inv_root_tau
    return hidden * normal_cdf, normal_cdf + hidden * density


def to_half(values):
    return lax.optimization_barrier(values.astype(jnp.bfloat16)).astype(jnp.float32)


def reference(tokens, cotangent, weight_in, weight_out):
    feat_block = D // N_ROW
    unit_block = FF // N_COL
    hidden = jnp.zeros((TOKENS, FF), jnp.float32)
    active_grad = jnp.zeros((TOKENS, FF), jnp.float32)
    for index in range(N_ROW):
        lower = index * feat_block
        upper = lower + feat_block
        hidden = hidden + to_half(jnp.dot(tokens[:, lower:upper], weight_in[lower:upper], preferred_element_type=jnp.float32))
        active_grad = active_grad + to_half(jnp.dot(cotangent[:, lower:upper], weight_out[lower:upper], preferred_element_type=jnp.float32))
    active_val, slope_val = gelu_pair(hidden)
    active = active_val.astype(jnp.bfloat16)
    hidden_grad = (active_grad * slope_val).astype(jnp.bfloat16)
    outputs = jnp.zeros((TOKENS, D), jnp.float32)
    token_gradient = jnp.zeros((TOKENS, D), jnp.float32)
    for index in range(N_COL):
        lower = index * unit_block
        upper = lower + unit_block
        outputs = outputs + to_half(jnp.dot(active[:, lower:upper], weight_out[:, lower:upper].T, preferred_element_type=jnp.float32))
        token_gradient = token_gradient + to_half(jnp.dot(hidden_grad[:, lower:upper], weight_in[:, lower:upper].T, preferred_element_type=jnp.float32))
    factor = 1.0 / TOKENS
    weight_in_gradient = jnp.zeros((D, FF), jnp.float32)
    weight_out_gradient = jnp.zeros((D, FF), jnp.float32)
    for group in range(N_DP):
        lower = group * TOKG
        upper = lower + TOKG
        weight_in_gradient = weight_in_gradient + to_half(jnp.dot(tokens[lower:upper].T, hidden_grad[lower:upper], preferred_element_type=jnp.float32) * factor)
        weight_out_gradient = weight_out_gradient + to_half(jnp.dot(cotangent[lower:upper].T, active[lower:upper], preferred_element_type=jnp.float32) * factor)
    return outputs.astype(jnp.bfloat16), token_gradient.astype(jnp.bfloat16), weight_in_gradient, weight_out_gradient
```

```python
import jax
import jax.numpy as jnp
from jax import lax
from jax.experimental import pallas as pl
from jax.experimental.pallas import tpu as pltpu
from jax.sharding import PartitionSpec as P

root_half = 0.7071067811865476
inv_root_tau = 0.3989422804014327
F32 = jnp.float32
BF16 = jnp.bfloat16


def gelu_pair(hidden):
    normal_cdf = 0.5 * (1.0 + lax.erf(hidden * root_half))
    density = jnp.exp(-0.5 * hidden * hidden) * inv_root_tau
    return (hidden * normal_cdf, normal_cdf + hidden * density)


def dot(left, right):
    return jnp.dot(left, right, preferred_element_type=F32)


def dot_across(left, right):
    return lax.dot_general(left, right, (((1,), (1,)), ((), ())), preferred_element_type=F32)


def swap(values, axis, bit):
    n = lax.axis_size(axis)
    return lax.ppermute(values, axis, [(i, i ^ bit) for i in range(n)])


def take_half(values, which):
    half = values.shape[0] // 2
    return lax.dynamic_slice_in_dim(values, which * half, half, 0)


def after(values, earlier):
    return lax.optimization_barrier((values, earlier[:8, :128]))[0]


def shift(values, by):
    n = lax.axis_size("dp")
    return lax.ppermute(values, "dp", [(i, (i + by) % n) for i in range(n)])


def gather_tokens(values):
    groups, cols = lax.axis_size("dp"), lax.axis_size("col")
    kept = values.shape[0] // cols
    if cols == 2:
        side = lax.axis_index("col")
        first = lax.dynamic_slice_in_dim(values, side * kept, kept, 0)
        second = lax.dynamic_slice_in_dim(values, (1 - side) * kept, kept, 0)
        rows = [first, second]
        moved = [shift(first, by) for by in range(1, groups)]
        for part in moved:
            rows += [part, swap(part, "col", 1)]
        return jnp.concatenate(rows)
    gathered = lax.all_gather(values, "dp", axis=0, tiled=False)
    order = (lax.axis_index("dp") - jnp.arange(groups)) % groups
    return gathered[order].reshape(-1, values.shape[1])


def core_sum(mine, others, weights):
    given = swap(dot(others, weights).astype(BF16), "row", 1)
    return (dot(mine, weights) + given.astype(F32)).astype(BF16)


def row_total(part):
    total, bit = part, 2
    while bit < lax.axis_size("row"):
        total = total.astype(BF16)
        total = total.astype(F32) + swap(total, "row", bit).astype(F32)
        bit *= 2
    return total


def column_sum(rows, right):
    groups, cols = lax.axis_size("dp") // 2, lax.axis_size("col")
    product = dot_across(rows, right).astype(BF16)
    kept = rows.shape[0] // (groups * cols)
    blocks = product.reshape(groups, cols, kept, -1)
    if cols == 2:
        given = swap(blocks[:, 1].reshape(groups * kept, -1), "col", 1)
        total = blocks[:, 0].reshape(groups * kept, -1).astype(F32) + given.astype(F32)
        return total.astype(BF16)
    part = lax.psum_scatter(blocks, "col", scatter_dimension=1, tiled=True)
    return part.reshape(groups * kept, -1)


def group_sum(mine, others, side):
    groups = lax.axis_size("dp")
    ordered = jnp.where(
        side == 0, jnp.concatenate([mine, others]), jnp.concatenate([others, mine])
    ).reshape(groups, -1, mine.shape[1])
    total = ordered[0].astype(F32)
    for received in [shift(ordered[by], -by) for by in range(1, groups)]:
        total = total + received.astype(F32)
    return total.astype(BF16)


def gradient_kernel(factor, left_a, left_b, right_a, right_b, out):
    out[...] = (dot(left_a[...], right_a[...]) + dot(left_b[...], right_b[...])) * factor


def weight_gradient(left_a, left_b, right_a, right_b, factor):
    (feats, half), units = left_a.shape, right_a.shape[1]
    wide = next((w for w in (640, 512, 384, 256, 128) if units % w == 0), units)
    left = pl.BlockSpec((feats, half), lambda i: (0, 0))
    right = pl.BlockSpec((half, wide), lambda i: (0, i))
    return pl.pallas_call(
        lambda *refs: gradient_kernel(factor, *refs),
        out_shape=jax.ShapeDtypeStruct((feats, units), F32),
        grid=(units // wide,),
        in_specs=[left, left, right, right],
        out_specs=pl.BlockSpec((feats, wide), lambda i: (0, i)),
        cost_estimate=pl.CostEstimate(
            flops=4 * feats * half * units,
            bytes_accessed=4 * feats * units + 4 * half * (feats + units),
            transcendentals=0,
        ),
        compiler_params=pltpu.CompilerParams(vmem_limit_bytes=24 * 2**20),
    )(left_a, left_b, right_a, right_b)


def shards(tokens, cotangent, weight_in, weight_out):
    groups = lax.axis_size("dp")
    factor = 1.0 / (tokens.shape[0] * groups)
    units = weight_in.shape[1] // groups
    start = lax.axis_index("dp") * units
    up = lax.dynamic_slice_in_dim(weight_in, start, units, 1)
    down = lax.dynamic_slice_in_dim(weight_out, start, units, 1)
    side = lax.axis_index("row") % 2

    tokens = gather_tokens(tokens)
    cotangent = gather_tokens(cotangent)
    token_mine, token_others = take_half(tokens, side), take_half(tokens, 1 - side)
    hidden_part = core_sum(token_mine, token_others, up)
    hidden = row_total(hidden_part)

    cotangent = after(cotangent, hidden_part)
    cot_mine, cot_others = take_half(cotangent, side), take_half(cotangent, 1 - side)
    grad_part = core_sum(cot_mine, cot_others, down)
    grad = row_total(grad_part)

    active_val, slope_val = gelu_pair(hidden)
    active = active_val.astype(BF16)
    active_other = swap(active, "row", 1)
    output_mine = column_sum(active, down)
    output_others = column_sum(active_other, down)
    outputs = group_sum(output_mine, output_others, side)
    weight_out_gradient = weight_gradient(cot_mine.T, cot_others.T, active, active_other, factor)

    hidden_grad = (grad * slope_val).astype(BF16)
    hidden_grad_other = swap(hidden_grad, "row", 1)
    token_grad_mine = column_sum(hidden_grad, up)
    token_grad_others = column_sum(hidden_grad_other, up)
    token_gradient = group_sum(token_grad_mine, token_grad_others, side)
    weight_in_gradient = weight_gradient(
        token_mine.T, token_others.T, hidden_grad, hidden_grad_other, factor
    )
    return (outputs, token_gradient, weight_in_gradient, weight_out_gradient)


def solution(mesh):
    return jax.shard_map(
        shards,
        mesh=mesh,
        in_specs=(P("dp", "row"), P("dp", "row"), P("row", "col"), P("row", "col")),
        out_specs=(
            P(("dp", "col"), "row"),
            P(("dp", "col"), "row"),
            P("row", ("col", "dp")),
            P("row", ("col", "dp")),
        ),
        check_vma=False,
    )
```

```python
import jax
import jax.numpy as jnp
from jax import lax
from jax.experimental import pallas as pl
from jax.experimental.pallas import tpu as pltpu
from jax.sharding import PartitionSpec as P


root_half = 0.7071067811865476
inv_root_tau = 0.3989422804014327
F32 = jnp.float32
BF16 = jnp.bfloat16


def gelu_pair(hidden):
    normal_cdf = 0.5 * (1.0 + lax.erf(hidden * root_half))
    density = jnp.exp(-0.5 * hidden * hidden) * inv_root_tau
    return (hidden * normal_cdf, normal_cdf + hidden * density)


def dot(left, right):
    return jnp.dot(left, right, preferred_element_type=F32)


def dot_across(left, right):
    return lax.dot_general(left, right, (((1,), (1,)), ((), ())), preferred_element_type=F32)


def swap(values, axis, bit):
    n = lax.axis_size(axis)
    return lax.ppermute(values, axis, [(i, i ^ bit) for i in range(n)])


def take_half(values, which):
    half = values.shape[0] // 2
    return lax.dynamic_slice_in_dim(values, which * half, half, 0)


def shift(values, by):
    n = lax.axis_size("dp")
    return lax.ppermute(values, "dp", [(i, (i + by) % n) for i in range(n)])


def gather_tokens(values):
    groups, cols = lax.axis_size("dp"), lax.axis_size("col")
    kept = values.shape[0] // cols
    if cols == 2:
        side = lax.axis_index("col")
        first = lax.dynamic_slice_in_dim(values, side * kept, kept, 0)
        second = lax.dynamic_slice_in_dim(values, (1 - side) * kept, kept, 0)
        moved = [shift(first, by) for by in range(1, groups)]
        moved = jnp.concatenate(moved)
        swapped = swap(moved, "col", 1)
        rows = [first, second]
        for i in range(groups - 1):
            rows += [moved[i * kept : (i + 1) * kept], swapped[i * kept : (i + 1) * kept]]
        return jnp.concatenate(rows)
    gathered = lax.all_gather(values, "dp", axis=0, tiled=False)
    order = (lax.axis_index("dp") - jnp.arange(groups)) % groups
    return gathered[order].reshape(-1, values.shape[1])


def core_sum(mine, others, weights):
    given = swap(dot(others, weights).astype(BF16), "row", 1)
    return (dot(mine, weights) + given.astype(F32)).astype(BF16)


def row_total(part):
    total, bit = part, 2
    while bit < lax.axis_size("row"):
        total = total.astype(BF16)
        total = total.astype(F32) + swap(total, "row", bit).astype(F32)
        bit *= 2
    return total


def column_sum(rows, right):
    groups, cols = lax.axis_size("dp") // 2, lax.axis_size("col")
    product = dot_across(rows, right).astype(BF16)
    kept = rows.shape[0] // (groups * cols)
    blocks = product.reshape(groups, cols, kept, -1)
    if cols == 2:
        given = swap(blocks[:, 1].reshape(groups * kept, -1), "col", 1)
        total = blocks[:, 0].reshape(groups * kept, -1).astype(F32) + given.astype(F32)
        return total.astype(BF16)
    part = lax.psum_scatter(blocks, "col", scatter_dimension=1, tiled=True)
    return part.reshape(groups * kept, -1)


def group_sum(mine, others, side):
    groups = lax.axis_size("dp")
    ordered = jnp.where(
        side == 0, jnp.concatenate([mine, others]), jnp.concatenate([others, mine])
    ).reshape(groups, -1, mine.shape[1])
    total = ordered[0].astype(F32)
    for received in [shift(ordered[by], -by) for by in range(1, groups)]:
        total = total + received.astype(F32)
    return total.astype(BF16)


def gradient_kernel(factor, left_a, left_b, right_a, right_b, out):
    out[...] = (dot(left_a[...], right_a[...]) + dot(left_b[...], right_b[...])) * factor


def weight_gradient(left_a, left_b, right_a, right_b, factor):
    (feats, half), units = left_a.shape, right_a.shape[1]
    wide = next((w for w in (640, 512, 384, 256, 128) if units % w == 0), units)
    left = pl.BlockSpec((feats, half), lambda i: (0, 0))
    right = pl.BlockSpec((half, wide), lambda i: (0, i))
    return pl.pallas_call(
        lambda *refs: gradient_kernel(factor, *refs),
        out_shape=jax.ShapeDtypeStruct((feats, units), F32),
        grid=(units // wide,),
        in_specs=[left, left, right, right],
        out_specs=pl.BlockSpec((feats, wide), lambda i: (0, i)),
        cost_estimate=pl.CostEstimate(
            flops=4 * feats * half * units,
            bytes_accessed=4 * feats * units + 4 * half * (feats + units),
            transcendentals=0,
        ),
        compiler_params=pltpu.CompilerParams(vmem_limit_bytes=24 * 2**20),
    )(left_a, left_b, right_a, right_b)


def shards(tokens, cotangent, weight_in, weight_out):
    groups = lax.axis_size("dp")
    factor = 1.0 / (tokens.shape[0] * groups)
    units = weight_in.shape[1] // groups
    start = lax.axis_index("dp") * units
    up = lax.dynamic_slice_in_dim(weight_in, start, units, 1)
    down = lax.dynamic_slice_in_dim(weight_out, start, units, 1)
    side = lax.axis_index("row") % 2

    tokens = gather_tokens(tokens)
    cotangent = gather_tokens(cotangent)
    token_mine, token_others = take_half(tokens, side), take_half(tokens, 1 - side)
    hidden_part = core_sum(token_mine, token_others, up)
    hidden = row_total(hidden_part)

    cot_mine, cot_others = take_half(cotangent, side), take_half(cotangent, 1 - side)
    grad_part = core_sum(cot_mine, cot_others, down)
    grad = row_total(grad_part)

    active_val, slope_val = gelu_pair(hidden)
    active, slope_val = lax.optimization_barrier((active_val.astype(BF16), slope_val))
    active_other = swap(active, "row", 1)
    output_mine = column_sum(active, down)
    output_others = column_sum(active_other, down)
    outputs = group_sum(output_mine, output_others, side)
    weight_out_gradient = weight_gradient(cot_mine.T, cot_others.T, active, active_other, factor)

    hidden_grad = (grad * slope_val).astype(BF16)
    hidden_grad_other = swap(hidden_grad, "row", 1)
    token_grad_mine = column_sum(hidden_grad, up)
    token_grad_others = column_sum(hidden_grad_other, up)
    token_gradient = group_sum(token_grad_mine, token_grad_others, side)
    weight_in_gradient = weight_gradient(
        token_mine.T, token_others.T, hidden_grad, hidden_grad_other, factor
    )
    return (outputs, token_gradient, weight_in_gradient, weight_out_gradient)


def solution(mesh):
    return jax.shard_map(
        shards,
        mesh=mesh,
        in_specs=(P("dp", "row"), P("dp", "row"), P("row", "col"), P("row", "col")),
        out_specs=(
            P(("dp", "col"), "row"),
            P(("dp", "col"), "row"),
            P("row", ("col", "dp")),
            P("row", ("col", "dp")),
        ),
        check_vma=False,
    )
```
